32 devices in a mesh: parts: 2 (over x), blk: 16 (over z, y, core).
Axes of the slice: x: 2, y: 2, z: 4, core: 2. Of those that a mesh axis runs over, the one named last changes fastest.
Arguments:
- queries: bfloat16 [256, 4096], P(('parts', 'blk')), parts along dimension 0, may hold values from -48 to 48
- key_cache: bfloat16 [8192, 512], P(('parts', 'blk')), parts along dimension 0, may hold values from -6 to 6
- value_cache: bfloat16 [8192, 512], P(('parts', 'blk')), parts along dimension 0, may hold values from -6 to 6
- tile_page: int32 [8192], P(('parts', 'blk')), parts along dimension 0, may hold values from 0 to 15, never falling along the last dimension, each value on 1 to 512 neighbouring positions
- row_last: int32 [256], P(('parts', 'blk')), parts along dimension 0, may hold values from 0 to 15, as said below
Outputs:
- attention_out: bfloat16 [256, 4096], P(('parts', 'blk')), parts along dimension 0
The draws below stay inside these ranges and needn't reach their ends.
There are 2 independent parts, one for each index of `parts`. The reference program is written for one: setup_inputs(seed, part) draws one part's arguments, and reference() takes and returns one part's arrays. A program takes and returns all parts, laid end to end along the dimension named above; each array names one. Nothing has to cross between parts.
Inputs may be any that keep to these rules, and one draw needn't show every extreme that they name: tile_page never falls along the tile tokens; every page of 0 to 15 has between 1 and 512 tokens, one exactly 512. row_last never falls along the text rows; the first row sees page 0 only and the last row sees every page.
All inputs are finite; a program needn't handle non-finite values.
Results may differ from the reference program's by a relative error of at most 0.00575.
Values may be sent and summed in bfloat16 or wider, within the bound.
No kernel may reach another device: no remote copies, remote signals or barrier semaphores. Data moves between devices by JAX's collectives and lax.ppermute only.
A program may use at most 64 MiB of HBM per device.

```python
import math
import jax
import jax.numpy as jnp
import numpy as np
from jax import lax

HEADS = 32
KV_HEADS = 4
HEAD_DIM = 128
TILE_DEV = 256
ROWS_DEV = 8
PAGES = 16
TILES = 4096
TEXT = 128
N_BLK = 16


def joint_draw(key):
    base_key = jax.random.fold_in(key, 7001)
    query_key, cache_key = jax.random.split(base_key, 2)
    group_size = HEADS // KV_HEADS
    cache_heads = jnp.clip(jax.random.normal(cache_key, (TILES, KV_HEADS, HEAD_DIM), jnp.float32), -6.0, 6.0)
    query_heads = jnp.clip(jax.random.normal(query_key, (TEXT, KV_HEADS, group_size, HEAD_DIM), jnp.float32), -6.0, 6.0)
    query_flat = query_heads.reshape(TEXT, HEADS * HEAD_DIM).astype(jnp.bfloat16)
    cache_flat = cache_heads.reshape(TILES, KV_HEADS * HEAD_DIM).astype(jnp.bfloat16)
    return (query_flat, cache_flat)


def draw_queries(key, part):
    return joint_draw(key)[0]


def draw_key_cache(key, part):
    return joint_draw(key)[1]


def draw_row_last(key, part):
    drawn = jax.random.randint(jax.random.fold_in(key, 9103), (TEXT,), 0, PAGES)
    ordered = jnp.sort(drawn)
    ordered = ordered.at[0].set(0).at[TEXT - 1].set(PAGES - 1)
    return ordered.astype(jnp.int32)


def levels(own_key, dims, shards, smallest, largest):
    gain, own = 1.0, jax.random.fold_in(own_key, 6)
    for dim, blocks in shards:
        draws = jnp.exp(jax.random.uniform(jax.random.fold_in(own, dim), (blocks,), jnp.float32, smallest / len(shards), largest / len(shards)))
        gain = gain * jnp.repeat(draws, dims[dim] // blocks).reshape([-1 if axis == dim else 1 for axis in range(len(dims))])
    return gain


def split_up(number_of, total, most, slope):
    weights = [(1 << 20) // math.isqrt(rank ** slope) + 1 for rank in range(2, number_of + 1)]
    spare, holding = total - most - (number_of - 1), [1] * (number_of - 1)
    while spare > 0:
        candidates = [i for i in range(number_of - 1) if holding[i] < most]
        whole, budget = sum([weights[i] for i in candidates]), spare
        for i in candidates:
            more = min(most - holding[i], max(1, budget * weights[i] // whole), spare)
            holding[i] = holding[i] + more
            spare = spare - more
    return np.array([most] + holding)


def ragged(own_key, count, total, limit, slope):
    if count == 2:
        one = jax.random.randint(own_key, (), max(1, total - limit), min(limit, total - 1) + 1)
        return jnp.stack([one, total - one])
    lengths = jnp.asarray(split_up(count, total, limit, slope), jnp.int32)
    twos = (count - 1) // 2
    donor, taker = lengths[1:1 + 2 * twos:2], lengths[2:2 + 2 * twos:2]
    slack = jnp.minimum(donor - 1, limit - taker)
    shifted = jax.random.randint(jax.random.fold_in(own_key, 1), (twos,), 0, 1 << 20) % (slack + 1)
    lengths = lengths.at[1:1 + 2 * twos:2].set(donor - shifted).at[2:2 + 2 * twos:2].set(taker + shifted)
    return lengths[jax.random.permutation(jax.random.fold_in(own_key, 2), count)]


def centred(stream_key, shape, spread, reach, pieces=(), dtype=jnp.bfloat16):
    values = jax.random.normal(stream_key, shape, jnp.float32) * spread
    if len(pieces) > 0:
        values = levels(stream_key, shape, pieces, -0.22, 0.18) * values
    return jnp.clip(values, min=-reach, max=reach).astype(dtype)


def setup_inputs(seed: int = 0, part: int = 0) -> dict:
    key_of = jax.random.split(jax.random.key(seed), 6)
    part_keys = jax.random.split(jax.random.fold_in(key_of[5], part), 6)
    return {
        "queries": draw_queries(jax.random.fold_in(jax.random.fold_in(key_of[5], part), 71), part),
        "key_cache": draw_key_cache(jax.random.fold_in(jax.random.fold_in(key_of[5], part), 71), part),
        "value_cache": centred(part_keys[2], (TILES, KV_HEADS * HEAD_DIM), 1.0, 6.0, ((0, 16),)),
        "tile_page": jnp.searchsorted(jnp.cumsum(ragged(part_keys[3], PAGES, TILES, 2 * TILE_DEV, 1)), jnp.arange(TILES), side="right").astype(jnp.int32),
        "row_last": draw_row_last(jax.random.fold_in(jax.random.fold_in(key_of[5], part), 71), part),
    }


NEGATIVE_FILL = -1e+30

def reference(queries, key_cache, value_cache, tile_page, row_last):
    group_size = HEADS // KV_HEADS
    score_scale = 1.0 / math.sqrt(HEAD_DIM)
    key_heads = key_cache.reshape(TILES, KV_HEADS, HEAD_DIM).astype(jnp.float32)
    value_heads = value_cache.reshape(TILES, KV_HEADS, HEAD_DIM).astype(jnp.float32)
    query_blocks = queries.reshape(N_BLK, ROWS_DEV, KV_HEADS, group_size, HEAD_DIM)
    last_blocks = row_last.reshape(N_BLK, ROWS_DEV)

    def attend_block(block_pair):
        query_rows, last_rows = block_pair
        scores = jnp.einsum('rkgd,tkd->rkgt', query_rows.astype(jnp.float32), key_heads) * score_scale
        visible = (tile_page[None, :] <= last_rows[:, None])[:, None, None, :]
        masked = jnp.where(visible, scores, NEGATIVE_FILL)
        row_top = lax.optimization_barrier(jnp.max(masked, axis=-1, keepdims=True))
        weights = jnp.where(visible, jnp.exp(scores - row_top), 0.0)
        weight_total = lax.optimization_barrier(jnp.sum(weights, axis=-1))
        rounded = lax.optimization_barrier(weights.astype(jnp.bfloat16))
        attended = jnp.einsum('rkgt,tkd->rkgd', rounded.astype(jnp.float32), value_heads)
        result = (attended / weight_total[..., None]).astype(jnp.bfloat16)
        return result.reshape(ROWS_DEV, HEADS * HEAD_DIM)
    blocks_out = lax.map(attend_block, (query_blocks, last_blocks))
    return blocks_out.reshape(TEXT, HEADS * HEAD_DIM)
```

```python
import functools
import math

import jax
import jax.numpy as jnp
from jax import lax
from jax.experimental import pallas as pl
from jax.experimental.pallas import tpu as pltpu
from jax.sharding import PartitionSpec as P

HEADS = 32
KV_HEADS = 4
GROUP = HEADS // KV_HEADS
HEAD_DIM = 128
WIDTH = HEADS * HEAD_DIM
KV_WIDTH = KV_HEADS * HEAD_DIM
LANES = 128
SHARE = 4
FAR = -(2.0**100)
EXP2_SCALE = math.log2(math.e) / math.sqrt(HEAD_DIM)


def swapped(block, distance):
    devices = lax.axis_size("blk")
    return lax.ppermute(block, "blk", [(i, i ^ distance) for i in range(devices)])


def partial_kernel(n_q, n_kv, *refs):
    q_refs, kv_refs, out_refs = refs[:n_q], refs[n_q : n_q + n_kv], refs[n_q + n_kv :]
    rows = q_refs[0].shape[0]
    tokens = kv_refs[0].shape[0] - 8
    lane = lax.broadcasted_iota(jnp.int32, (rows, LANES), 1)
    token_lane = lax.broadcasted_iota(jnp.int32, (tokens, LANES), 1).astype(jnp.float32)
    pick = jnp.where(
        lax.broadcasted_iota(jnp.int32, (8, LANES), 0) == 0, 1.0, 0.0
    ).astype(jnp.bfloat16)
    hides = []
    for ref in kv_refs:
        pages = ref[tokens:, :tokens]
        column = lax.dot_general(
            pages, pick, (((0,), (0,)), ((), ())), preferred_element_type=jnp.float32
        )
        hides.append(jnp.where(column > token_lane, FAR, 0.0).astype(jnp.bfloat16))
    ones = jnp.ones((tokens, LANES), jnp.bfloat16)
    stats = [[jnp.zeros((rows, LANES), jnp.float32)] * 3 for _ in range(n_q)]
    last = [ref[:, WIDTH:].astype(jnp.float32) for ref in q_refs]
    for kv in range(KV_HEADS):
        parts = []
        for i, ref in enumerate(q_refs):
            for g in range(GROUP):
                head = kv * GROUP + g
                q = ref[:, head * HEAD_DIM : (head + 1) * HEAD_DIM].astype(jnp.float32)
                parts.append(jnp.concatenate([q, last[i]], axis=1))
        q_all = jnp.concatenate(parts, axis=0).astype(jnp.bfloat16)
        scores = []
        for ref, hide in zip(kv_refs, hides):
            k = ref[:tokens, kv * HEAD_DIM : (kv + 1) * HEAD_DIM]
            scores.append(
                lax.dot_general(
                    q_all,
                    jnp.concatenate([k, hide], axis=1),
                    (((1,), (1,)), ((), ())),
                    preferred_element_type=jnp.float32,
                )
            )
        top = functools.reduce(
            jnp.maximum, [jnp.max(s, axis=1, keepdims=True) for s in scores]
        )
        top = top.astype(jnp.bfloat16).astype(jnp.float32)
        total = None
        for s, ref in zip(scores, kv_refs):
            weights = jnp.exp2((s - top) * EXP2_SCALE).astype(jnp.bfloat16)
            start = KV_WIDTH + kv * HEAD_DIM
            v = jnp.concatenate([ref[:tokens, start : start + HEAD_DIM], ones], axis=1)
            part = jnp.dot(weights, v, preferred_element_type=jnp.float32)
            total = part if total is None else total + part
        for i, ref in enumerate(out_refs):
            for g in range(GROUP):
                head = kv * GROUP + g
                at = slice((i * GROUP + g) * rows, (i * GROUP + g + 1) * rows)
                ref[:, head * HEAD_DIM : (head + 1) * HEAD_DIM] = total[
                    at, :HEAD_DIM
                ].astype(jnp.bfloat16)
                mass = total[at, HEAD_DIM:]
                high = mass.astype(jnp.bfloat16).astype(jnp.float32)
                here = lane == head
                stats[i][0] = jnp.where(here, top[at], stats[i][0])
                stats[i][1] = jnp.where(here, high, stats[i][1])
                stats[i][2] = jnp.where(here, mass - high, stats[i][2])
    for i, ref in enumerate(out_refs):
        for j in range(3):
            ref[:, WIDTH + j * LANES : WIDTH + (j + 1) * LANES] = stats[i][j].astype(
                jnp.bfloat16
            )


def partial_call(q_blocks, kv_blocks):
    n_q, n_kv = len(q_blocks), len(kv_blocks)
    rows = q_blocks[0].shape[0]
    vmem = pl.BlockSpec(memory_space=pltpu.VMEM)
    return pl.pallas_call(
        functools.partial(partial_kernel, n_q, n_kv),
        out_shape=[jax.ShapeDtypeStruct((rows, WIDTH + 3 * LANES), jnp.bfloat16)] * n_q,
        in_specs=[vmem] * (n_q + n_kv),
        out_specs=[vmem] * n_q,
    )(*q_blocks, *kv_blocks)


def merge_kernel(n, *refs):
    parts, out_ref = refs[:n], refs[n]
    tops, masses = [], []
    for ref in parts:
        stat = [
            ref[:, WIDTH + j * LANES : WIDTH + (j + 1) * LANES].astype(jnp.float32)
            for j in range(3)
        ]
        tops.append(stat[0])
        masses.append(stat[1] + stat[2])
    top = functools.reduce(jnp.maximum, tops)
    factors = [jnp.exp2((t - top) * EXP2_SCALE) for t in tops]
    total = functools.reduce(jnp.add, [f * m for f, m in zip(factors, masses)])
    shares = [f / total for f in factors]
    for head in range(HEADS):
        at = slice(head * HEAD_DIM, (head + 1) * HEAD_DIM)
        value = functools.reduce(
            jnp.add,
            [
                share[:, head : head + 1] * ref[:, at].astype(jnp.float32)
                for share, ref in zip(shares, parts)
            ],
        )
        out_ref[:, at] = value.astype(jnp.bfloat16)


def merge_call(parts):
    rows = parts[0].shape[0]
    vmem = pl.BlockSpec(memory_space=pltpu.VMEM)
    return pl.pallas_call(
        functools.partial(merge_kernel, len(parts)),
        out_shape=jax.ShapeDtypeStruct((rows, WIDTH), jnp.bfloat16),
        in_specs=[vmem] * len(parts),
        out_specs=vmem,
    )(*parts)


def shards(queries, key_cache, value_cache, tile_page, row_last):
    groups = lax.axis_size("blk") // SHARE
    rows, tokens = queries.shape[0], key_cache.shape[0]
    page_lane = lax.broadcasted_iota(jnp.int32, (rows, LANES), 1)
    seen = (page_lane == row_last[:, None]).astype(jnp.bfloat16)
    own_q = jnp.concatenate([queries, seen], axis=1)
    pages = jnp.pad(
        tile_page.astype(jnp.bfloat16)[None, :], ((0, 7), (0, 2 * KV_WIDTH - tokens))
    )
    own_kv = jnp.concatenate(
        [jnp.concatenate([key_cache, value_cache], axis=1), pages], axis=0
    )
    across = swapped(own_kv, 2)
    kv_blocks = [own_kv, swapped(own_kv, 1), across, swapped(across, 1)]
    q_blocks = [own_q] + [swapped(own_q, SHARE * d) for d in range(1, groups)]
    partials = []
    for start in range(0, groups, 4):
        partials += partial_call(q_blocks[start : start + 4], kv_blocks)
    parts = [partials[0]] + [
        swapped(partials[d], SHARE * d) for d in range(1, groups)
    ]
    return merge_call(parts)


def solution(mesh):
    placed = (
        P(("parts", "blk"), None),
        P(("parts", "blk"), None),
        P(("parts", "blk"), None),
        P(("parts", "blk")),
        P(("parts", "blk")),
    )
    return jax.shard_map(
        shards, mesh=mesh, in_specs=placed, out_specs=P(("parts", "blk"), None), check_vma=False
    )
```

```python
import functools
import math

import jax
import jax.numpy as jnp
from jax import lax
from jax.experimental import pallas as pl
from jax.experimental.pallas import tpu as pltpu
from jax.sharding import PartitionSpec as P


HEADS = 32
KV_HEADS = 4
GROUP = HEADS // KV_HEADS
HEAD_DIM = 128
WIDTH = HEADS * HEAD_DIM
LANES = 128
SHARE = 4
FAR = -(2.0**100)
EXP2_SCALE = math.log2(math.e) / math.sqrt(HEAD_DIM)


def swapped(block, distance):
    devices = lax.axis_size("blk")
    return lax.ppermute(block, "blk", [(i, i ^ distance) for i in range(devices)])


def weights_kernel(n_q, n_kv, *refs):
    q_refs, k_refs = refs[:n_q], refs[n_q : n_q + n_kv]
    page_refs = refs[n_q + n_kv : n_q + 2 * n_kv]
    weight_ref, top_ref = refs[n_q + 2 * n_kv :]
    rows, tokens = q_refs[0].shape[0], k_refs[0].shape[0]
    lane = lax.broadcasted_iota(jnp.int32, (rows, LANES), 1)
    token_lane = lax.broadcasted_iota(jnp.int32, (tokens, LANES), 1).astype(jnp.float32)
    pick = jnp.where(
        lax.broadcasted_iota(jnp.int32, (8, LANES), 0) == 0, 1.0, 0.0
    ).astype(jnp.bfloat16)
    hides = []
    for ref in page_refs:
        pages = jnp.broadcast_to(ref[...], (8, tokens)).astype(jnp.float32)
        column = lax.dot_general(
            pages.astype(jnp.bfloat16),
            pick,
            (((0,), (0,)), ((), ())),
            preferred_element_type=jnp.float32,
        )
        hides.append(jnp.where(column > token_lane, FAR, 0.0).astype(jnp.bfloat16))
    tops = [jnp.zeros((rows, LANES), jnp.float32)] * n_q
    last = [ref[:, WIDTH:].astype(jnp.float32) for ref in q_refs]
    count = n_q * GROUP * rows
    for kv in range(KV_HEADS):
        parts = []
        for i, ref in enumerate(q_refs):
            for g in range(GROUP):
                head = kv * GROUP + g
                q = ref[:, head * HEAD_DIM : (head + 1) * HEAD_DIM].astype(jnp.float32)
                parts.append(jnp.concatenate([q, last[i]], axis=1))
        q_all = jnp.concatenate(parts, axis=0).astype(jnp.bfloat16)
        scores = []
        for ref, hide in zip(k_refs, hides):
            k = ref[:, kv * HEAD_DIM : (kv + 1) * HEAD_DIM]
            scores.append(
                lax.dot_general(
                    q_all,
                    jnp.concatenate([k, hide], axis=1),
                    (((1,), (1,)), ((), ())),
                    preferred_element_type=jnp.float32,
                )
            )
        top = functools.reduce(
            jnp.maximum, [jnp.max(s, axis=1, keepdims=True) for s in scores]
        )
        top = top.astype(jnp.bfloat16).astype(jnp.float32)
        for j, s in enumerate(scores):
            weight_ref[
                kv * count : (kv + 1) * count, j * tokens : (j + 1) * tokens
            ] = jnp.exp2((s - top) * EXP2_SCALE).astype(jnp.bfloat16)
        for i in range(n_q):
            for g in range(GROUP):
                at = slice((i * GROUP + g) * rows, (i * GROUP + g + 1) * rows)
                tops[i] = jnp.where(lane == kv * GROUP + g, top[at], tops[i])
    for i in range(n_q):
        top_ref[i * rows : (i + 1) * rows, :] = tops[i]


def values_kernel(n_q, n_kv, *refs):
    weight_ref, top_ref = refs[:2]
    v_refs, out_refs = refs[2 : 2 + n_kv], refs[2 + n_kv :]
    rows, tokens = out_refs[0].shape[0], v_refs[0].shape[0]
    count = n_q * GROUP * rows
    lane = lax.broadcasted_iota(jnp.int32, (rows, LANES), 1)
    ones = jnp.ones((tokens, LANES), jnp.bfloat16)
    stats = [[jnp.zeros((rows, LANES), jnp.float32)] * 2 for _ in range(n_q)]
    for kv in range(KV_HEADS):
        total = None
        for j, ref in enumerate(v_refs):
            weights = weight_ref[
                kv * count : (kv + 1) * count, j * tokens : (j + 1) * tokens
            ]
            v = jnp.concatenate(
                [ref[:, kv * HEAD_DIM : (kv + 1) * HEAD_DIM], ones], axis=1
            )
            part = jnp.dot(weights, v, preferred_element_type=jnp.float32)
            total = part if total is None else total + part
        for i, ref in enumerate(out_refs):
            for g in range(GROUP):
                head = kv * GROUP + g
                at = slice((i * GROUP + g) * rows, (i * GROUP + g + 1) * rows)
                ref[:, head * HEAD_DIM : (head + 1) * HEAD_DIM] = total[
                    at, :HEAD_DIM
                ].astype(jnp.bfloat16)
                mass = total[at, HEAD_DIM:]
                high = mass.astype(jnp.bfloat16).astype(jnp.float32)
                here = lane == head
                stats[i][0] = jnp.where(here, high, stats[i][0])
                stats[i][1] = jnp.where(here, mass - high, stats[i][1])
    for i, ref in enumerate(out_refs):
        columns = [top_ref[i * rows : (i + 1) * rows, :], *stats[i]]
        for j, column in enumerate(columns):
            ref[:, WIDTH + j * LANES : WIDTH + (j + 1) * LANES] = column.astype(
                jnp.bfloat16
            )


VMEM_BLOCK = pl.BlockSpec(memory_space=pltpu.VMEM)


def weights_call(q_blocks, k_blocks, page_blocks):
    n_q, n_kv = len(q_blocks), len(k_blocks)
    rows, tokens = q_blocks[0].shape[0], k_blocks[0].shape[0]
    return pl.pallas_call(
        functools.partial(weights_kernel, n_q, n_kv),
        out_shape=[
            jax.ShapeDtypeStruct((n_q * HEADS * rows, n_kv * tokens), jnp.bfloat16),
            jax.ShapeDtypeStruct((n_q * rows, LANES), jnp.float32),
        ],
        in_specs=[VMEM_BLOCK] * (n_q + 2 * n_kv),
        out_specs=[VMEM_BLOCK] * 2,
        compiler_params=pltpu.CompilerParams(vmem_limit_bytes=24 << 20),
    )(*q_blocks, *k_blocks, *page_blocks)


def values_call(weights, tops, v_blocks, n_q):
    n_kv = len(v_blocks)
    rows = tops.shape[0] // n_q
    return pl.pallas_call(
        functools.partial(values_kernel, n_q, n_kv),
        out_shape=[jax.ShapeDtypeStruct((rows, WIDTH + 3 * LANES), jnp.bfloat16)] * n_q,
        in_specs=[VMEM_BLOCK] * (2 + n_kv),
        out_specs=[VMEM_BLOCK] * n_q,
        compiler_params=pltpu.CompilerParams(vmem_limit_bytes=24 << 20),
    )(weights, tops, *v_blocks)


def merge_kernel(n, *refs):
    parts, out_ref = refs[:n], refs[n]
    tops, masses = [], []
    for ref in parts:
        stat = [
            ref[:, WIDTH + j * LANES : WIDTH + (j + 1) * LANES].astype(jnp.float32)
            for j in range(3)
        ]
        tops.append(stat[0])
        masses.append(stat[1] + stat[2])
    top = functools.reduce(jnp.maximum, tops)
    factors = [jnp.exp2((t - top) * EXP2_SCALE) for t in tops]
    total = functools.reduce(jnp.add, [f * m for f, m in zip(factors, masses)])
    shares = [f / total for f in factors]
    for head in range(HEADS):
        at = slice(head * HEAD_DIM, (head + 1) * HEAD_DIM)
        value = functools.reduce(
            jnp.add,
            [
                share[:, head : head + 1] * ref[:, at].astype(jnp.float32)
                for share, ref in zip(shares, parts)
            ],
        )
        out_ref[:, at] = value.astype(jnp.bfloat16)


def merge_call(parts):
    rows = parts[0].shape[0]
    return pl.pallas_call(
        functools.partial(merge_kernel, len(parts)),
        out_shape=jax.ShapeDtypeStruct((rows, WIDTH), jnp.bfloat16),
        in_specs=[VMEM_BLOCK] * len(parts),
        out_specs=VMEM_BLOCK,
        compiler_params=pltpu.CompilerParams(vmem_limit_bytes=8 << 20),
    )(*parts)


def pooled(block):
    across = swapped(block, 2)
    beside = swapped(block, 1)
    return [block, beside, across, swapped(across, 1)]


def attend(queries, key_cache, value_cache, tile_page, row_last):
    groups = lax.axis_size("blk") // SHARE
    rows = queries.shape[0]
    page_lane = lax.broadcasted_iota(jnp.int32, (rows, LANES), 1)
    seen = (page_lane == row_last[:, None]).astype(jnp.bfloat16)
    own_q = jnp.concatenate([queries, seen], axis=1)
    k_blocks = pooled(key_cache)
    v_blocks = pooled(value_cache)
    page_blocks = pooled(tile_page.reshape(1, -1))
    q_blocks = [own_q] + [swapped(own_q, SHARE * d) for d in range(1, groups)]
    partials = []
    for start in range(0, groups, 4):
        some = q_blocks[start : start + 4]
        weights, tops = weights_call(some, k_blocks, page_blocks)
        partials += values_call(weights, tops, v_blocks, len(some))
    parts = [partials[0]] + [swapped(partials[d], SHARE * d) for d in range(1, groups)]
    return merge_call(parts)


def solution(mesh):
    placed = (
        P(("parts", "blk"), None),
        P(("parts", "blk"), None),
        P(("parts", "blk"), None),
        P(("parts", "blk")),
        P(("parts", "blk")),
    )
    return jax.shard_map(
        attend, mesh=mesh, in_specs=placed, out_specs=P(("parts", "blk"), None), check_vma=False
    )
```

```python
import functools
import math

import jax
import jax.numpy as jnp
from jax import lax
from jax.experimental import pallas as pl
from jax.experimental.pallas import tpu as pltpu
from jax.sharding import PartitionSpec as P


HEADS = 32
KV_HEADS = 4
GROUP = HEADS // KV_HEADS
HEAD_DIM = 128
WIDTH = HEADS * HEAD_DIM
KV_WIDTH = KV_HEADS * HEAD_DIM
LANES = 128
SHARE = 4
FAR = -(2.0**100)
EXP2_SCALE = math.log2(math.e) / math.sqrt(HEAD_DIM)


def swapped(block, distance):
    devices = lax.axis_size("blk")
    return lax.ppermute(block, "blk", [(i, i ^ distance) for i in range(devices)])


VMEM_BLOCK = pl.BlockSpec(memory_space=pltpu.VMEM)


HBM_BLOCK = pl.BlockSpec(memory_space=pltpu.MemorySpace.HBM)


def in_hbm(array):
    return pltpu.with_memory_space_constraint(array, pltpu.MemorySpace.HBM)


def stage_kernel(
    q_ref, k_ref, v_ref, page_ref, last_ref, q_out, k_out, v_out, page, last, sems
):
    rows, tokens = q_ref.shape[0], k_ref.shape[0]
    moves = (
        (last_ref, last),
        (page_ref, page),
        (q_ref, q_out.at[:, :WIDTH]),
        (k_ref, k_out.at[:tokens, :]),
        (v_ref, v_out),
    )
    copies = [pltpu.make_async_copy(s, d, sems.at[i]) for i, (s, d) in enumerate(moves)]
    for copy in copies:
        copy.start()
    row = lax.broadcasted_iota(jnp.int32, (rows, LANES), 0)
    lane = lax.broadcasted_iota(jnp.int32, (rows, LANES), 1)
    copies[0].wait()
    seen = functools.reduce(
        jnp.logical_or, [(row == r) & (lane == last[r]) for r in range(rows)]
    )
    q_out[:, WIDTH:] = jnp.where(seen, 1.0, 0.0).astype(jnp.bfloat16)
    copies[1].wait()
    filled = jnp.broadcast_to(page[...], (8, tokens)).astype(jnp.float32)
    k_out[tokens:, :tokens] = filled.astype(jnp.bfloat16)
    k_out[tokens:, tokens:] = jnp.zeros((8, k_out.shape[1] - tokens), jnp.bfloat16)
    for copy in copies[2:]:
        copy.wait()


def stage_call(row_last, queries, key_cache, value_cache, pages):
    rows, tokens = queries.shape[0], key_cache.shape[0]
    return pl.pallas_call(
        stage_kernel,
        out_shape=[
            jax.ShapeDtypeStruct((rows, WIDTH + LANES), jnp.bfloat16),
            jax.ShapeDtypeStruct((tokens + 8, KV_WIDTH), jnp.bfloat16),
            jax.ShapeDtypeStruct(value_cache.shape, jnp.bfloat16),
        ],
        in_specs=[HBM_BLOCK] * 5,
        out_specs=[VMEM_BLOCK] * 3,
        scratch_shapes=[
            pltpu.VMEM((1, tokens), jnp.int32),
            pltpu.SMEM((rows,), jnp.int32),
            pltpu.SemaphoreType.DMA((5,)),
        ],
        compiler_params=pltpu.CompilerParams(vmem_limit_bytes=8 << 20),
    )(*map(in_hbm, (queries, key_cache, value_cache, pages, row_last)))


def weights_kernel(n_q, n_kv, *refs):
    q_refs, k_refs = refs[:n_q], refs[n_q : n_q + n_kv]
    weight_ref, top_ref = refs[n_q + n_kv :]
    rows, tokens = q_refs[0].shape[0], k_refs[0].shape[0] - 8
    lane = lax.broadcasted_iota(jnp.int32, (rows, LANES), 1)
    token_lane = lax.broadcasted_iota(jnp.int32, (tokens, LANES), 1).astype(jnp.float32)
    pick = jnp.where(
        lax.broadcasted_iota(jnp.int32, (8, LANES), 0) == 0, 1.0, 0.0
    ).astype(jnp.bfloat16)
    hides = []
    for ref in k_refs:
        column = lax.dot_general(
            ref[tokens:, :tokens],
            pick,
            (((0,), (0,)), ((), ())),
            preferred_element_type=jnp.float32,
        )
        hides.append(jnp.where(column > token_lane, FAR, 0.0).astype(jnp.bfloat16))
    tops = [jnp.zeros((rows, LANES), jnp.float32)] * n_q
    last = [ref[:, WIDTH:].astype(jnp.float32) for ref in q_refs]
    count = n_q * GROUP * rows
    for kv in range(KV_HEADS):
        parts = []
        for i, ref in enumerate(q_refs):
            for g in range(GROUP):
                head = kv * GROUP + g
                q = ref[:, head * HEAD_DIM : (head + 1) * HEAD_DIM].astype(jnp.float32)
                parts.append(jnp.concatenate([q, last[i]], axis=1))
        q_all = jnp.concatenate(parts, axis=0).astype(jnp.bfloat16)
        scores = []
        for ref, hide in zip(k_refs, hides):
            k = ref[:tokens, kv * HEAD_DIM : (kv + 1) * HEAD_DIM]
            scores.append(
                lax.dot_general(
                    q_all,
                    jnp.concatenate([k, hide], axis=1),
                    (((1,), (1,)), ((), ())),
                    preferred_element_type=jnp.float32,
                )
            )
        top = functools.reduce(
            jnp.maximum, [jnp.max(s, axis=1, keepdims=True) for s in scores]
        )
        top = top.astype(jnp.bfloat16).astype(jnp.float32)
        for j, s in enumerate(scores):
            weight_ref[
                kv * count : (kv + 1) * count, j * tokens : (j + 1) * tokens
            ] = jnp.exp2((s - top) * EXP2_SCALE).astype(jnp.bfloat16)
        for i in range(n_q):
            for g in range(GROUP):
                at = slice((i * GROUP + g) * rows, (i * GROUP + g + 1) * rows)
                tops[i] = jnp.where(lane == kv * GROUP + g, top[at], tops[i])
    for i in range(n_q):
        top_ref[i * rows : (i + 1) * rows, :] = tops[i]


def values_kernel(n_q, n_kv, *refs):
    weight_ref, top_ref = refs[:2]
    v_refs, out_refs = refs[2 : 2 + n_kv], refs[2 + n_kv :]
    rows, tokens = out_refs[0].shape[0], v_refs[0].shape[0]
    count = n_q * GROUP * rows
    lane = lax.broadcasted_iota(jnp.int32, (rows, LANES), 1)
    ones = jnp.ones((tokens, LANES), jnp.bfloat16)
    stats = [top_ref[i * rows : (i + 1) * rows, :] for i in range(n_q)]
    for kv in range(KV_HEADS):
        total = None
        for j, ref in enumerate(v_refs):
            weights = weight_ref[
                kv * count : (kv + 1) * count, j * tokens : (j + 1) * tokens
            ]
            v = jnp.concatenate(
                [ref[:, kv * HEAD_DIM : (kv + 1) * HEAD_DIM], ones], axis=1
            )
            part = jnp.dot(weights, v, preferred_element_type=jnp.float32)
            total = part if total is None else total + part
        for i, ref in enumerate(out_refs):
            for g in range(GROUP):
                head = kv * GROUP + g
                at = slice((i * GROUP + g) * rows, (i * GROUP + g + 1) * rows)
                ref[:, head * HEAD_DIM : (head + 1) * HEAD_DIM] = total[
                    at, :HEAD_DIM
                ].astype(jnp.bfloat16)
                mass = total[at, HEAD_DIM:]
                high = mass.astype(jnp.bfloat16).astype(jnp.float32)
                stats[i] = jnp.where(lane == HEADS + head, high, stats[i])
                stats[i] = jnp.where(lane == 2 * HEADS + head, mass - high, stats[i])
    for stat, ref in zip(stats, out_refs):
        ref[:, WIDTH:] = stat.astype(jnp.bfloat16)


def weights_call(q_blocks, k_blocks):
    n_q, n_kv = len(q_blocks), len(k_blocks)
    rows, tokens = q_blocks[0].shape[0], k_blocks[0].shape[0] - 8
    return pl.pallas_call(
        functools.partial(weights_kernel, n_q, n_kv),
        out_shape=[
            jax.ShapeDtypeStruct((n_q * HEADS * rows, n_kv * tokens), jnp.bfloat16),
            jax.ShapeDtypeStruct((n_q * rows, LANES), jnp.float32),
        ],
        in_specs=[VMEM_BLOCK] * (n_q + n_kv),
        out_specs=[VMEM_BLOCK] * 2,
        compiler_params=pltpu.CompilerParams(vmem_limit_bytes=24 << 20),
    )(*q_blocks, *k_blocks)


def values_call(weights, tops, v_blocks, n_q):
    n_kv = len(v_blocks)
    rows = tops.shape[0] // n_q
    return pl.pallas_call(
        functools.partial(values_kernel, n_q, n_kv),
        out_shape=[jax.ShapeDtypeStruct((rows, WIDTH + LANES), jnp.bfloat16)] * n_q,
        in_specs=[VMEM_BLOCK] * (2 + n_kv),
        out_specs=[VMEM_BLOCK] * n_q,
        compiler_params=pltpu.CompilerParams(vmem_limit_bytes=24 << 20),
    )(weights, tops, *v_blocks)


def merge_kernel(n, *refs):
    parts, out_ref = refs[:n], refs[n]
    tops, masses = [], []
    for ref in parts:
        stat = ref[:, WIDTH:].astype(jnp.float32)
        tops.append(stat)
        masses.append(
            pltpu.roll(stat, LANES - HEADS, 1) + pltpu.roll(stat, LANES - 2 * HEADS, 1)
        )
    top = functools.reduce(jnp.maximum, tops)
    factors = [jnp.exp2((t - top) * EXP2_SCALE) for t in tops]
    total = functools.reduce(jnp.add, [f * m for f, m in zip(factors, masses)])
    shares = [f / total for f in factors]
    for head in range(HEADS):
        at = slice(head * HEAD_DIM, (head + 1) * HEAD_DIM)
        value = functools.reduce(
            jnp.add,
            [
                share[:, head : head + 1] * ref[:, at].astype(jnp.float32)
                for share, ref in zip(shares, parts)
            ],
        )
        out_ref[:, at] = value.astype(jnp.bfloat16)


def merge_call(parts):
    rows = parts[0].shape[0]
    return pl.pallas_call(
        functools.partial(merge_kernel, len(parts)),
        out_shape=jax.ShapeDtypeStruct((rows, WIDTH), jnp.bfloat16),
        in_specs=[VMEM_BLOCK] * len(parts),
        out_specs=VMEM_BLOCK,
        compiler_params=pltpu.CompilerParams(vmem_limit_bytes=8 << 20),
    )(*parts)


def pooled(block, own):
    across = swapped(block, 2)
    beside = swapped(block, 1)
    return [own, beside, across, swapped(across, 1)]


def attend(queries, key_cache, value_cache, tile_page, row_last):
    groups = lax.axis_size("blk") // SHARE
    pages = tile_page.reshape(1, -1)
    own_q, own_k, own_v = stage_call(row_last, queries, key_cache, value_cache, pages)
    k_blocks = pooled(own_k, own_k)
    v_blocks = pooled(value_cache, own_v)
    q_blocks = [own_q] + [swapped(own_q, SHARE * d) for d in range(1, groups)]
    partials = []
    for start in range(0, groups, 4):
        some = q_blocks[start : start + 4]
        weights, tops = weights_call(some, k_blocks)
        partials += values_call(weights, tops, v_blocks, len(some))
    parts = [partials[0]] + [swapped(partials[d], SHARE * d) for d in range(1, groups)]
    return merge_call(parts)


def solution(mesh):
    placed = (
        P(("parts", "blk"), None),
        P(("parts", "blk"), None),
        P(("parts", "blk"), None),
        P(("parts", "blk")),
        P(("parts", "blk")),
    )
    return jax.shard_map(
        attend, mesh=mesh, in_specs=placed, out_specs=P(("parts", "blk"), None), check_vma=False
    )
```

```python
import functools
import math

import jax
import jax.numpy as jnp
from jax import lax
from jax.experimental import pallas as pl
from jax.experimental.pallas import tpu as pltpu
from jax.sharding import PartitionSpec as P


HEADS = 32
KV_HEADS = 4
GROUP = HEADS // KV_HEADS
HEAD_DIM = 128
WIDTH = HEADS * HEAD_DIM
LANES = 128
SHARE = 4
FAR = -(2.0**100)
EXP2_SCALE = math.log2(math.e) / math.sqrt(HEAD_DIM)


def swapped(block, distance):
    devices = lax.axis_size("blk")
    return lax.ppermute(block, "blk", [(i, i ^ distance) for i in range(devices)])


VMEM_BLOCK = pl.BlockSpec(memory_space=pltpu.VMEM)


HBM_BLOCK = pl.BlockSpec(memory_space=pltpu.MemorySpace.HBM)


def in_hbm(array):
    return pltpu.with_memory_space_constraint(array, pltpu.MemorySpace.HBM)


def stage_kernel(
    q_ref, k_ref, v_ref, page_ref, last_ref, q_out, k_out, v_out, page_out, last, sems
):
    rows = q_ref.shape[0]
    moves = (
        (last_ref, last),
        (q_ref, q_out.at[:, :WIDTH]),
        (page_ref, page_out),
        (k_ref, k_out),
        (v_ref, v_out),
    )
    copies = [pltpu.make_async_copy(s, d, sems.at[i]) for i, (s, d) in enumerate(moves)]
    for copy in copies:
        copy.start()
    row = lax.broadcasted_iota(jnp.int32, (rows, LANES), 0)
    lane = lax.broadcasted_iota(jnp.int32, (rows, LANES), 1)
    copies[0].wait()
    seen = functools.reduce(
        jnp.logical_or, [(row == r) & (lane == last[r]) for r in range(rows)]
    )
    q_out[:, WIDTH:] = jnp.where(seen, 1.0, 0.0).astype(jnp.bfloat16)
    for copy in copies[1:]:
        copy.wait()


def stage_call(row_last, queries, key_cache, value_cache, pages):
    rows = queries.shape[0]
    return pl.pallas_call(
        stage_kernel,
        out_shape=[
            jax.ShapeDtypeStruct((rows, WIDTH + LANES), jnp.bfloat16),
            jax.ShapeDtypeStruct(key_cache.shape, jnp.bfloat16),
            jax.ShapeDtypeStruct(value_cache.shape, jnp.bfloat16),
            jax.ShapeDtypeStruct(pages.shape, jnp.int32),
        ],
        in_specs=[HBM_BLOCK] * 5,
        out_specs=[VMEM_BLOCK] * 4,
        scratch_shapes=[pltpu.SMEM((rows,), jnp.int32), pltpu.SemaphoreType.DMA((5,))],
        compiler_params=pltpu.CompilerParams(vmem_limit_bytes=8 << 20),
    )(*map(in_hbm, (queries, key_cache, value_cache, pages, row_last)))


def weights_kernel(n_q, n_kv, *refs):
    q_refs, k_refs = refs[:n_q], refs[n_q : n_q + n_kv]
    page_refs = refs[n_q + n_kv : n_q + 2 * n_kv]
    weight_ref, top_ref = refs[n_q + 2 * n_kv :]
    rows, tokens = q_refs[0].shape[0], k_refs[0].shape[0]
    lane = lax.broadcasted_iota(jnp.int32, (rows, LANES), 1)
    token_lane = lax.broadcasted_iota(jnp.int32, (tokens, LANES), 1).astype(jnp.float32)
    pick = jnp.where(
        lax.broadcasted_iota(jnp.int32, (8, LANES), 0) == 0, 1.0, 0.0
    ).astype(jnp.bfloat16)
    hides = []
    for ref in page_refs:
        pages = jnp.broadcast_to(ref[...], (8, tokens)).astype(jnp.float32)
        column = lax.dot_general(
            pages.astype(jnp.bfloat16),
            pick,
            (((0,), (0,)), ((), ())),
            preferred_element_type=jnp.float32,
        )
        hides.append(jnp.where(column > token_lane, FAR, 0.0).astype(jnp.bfloat16))
    tops = [jnp.zeros((rows, LANES), jnp.float32)] * n_q
    last = [ref[:, WIDTH:].astype(jnp.float32) for ref in q_refs]
    count = n_q * GROUP * rows
    for kv in range(KV_HEADS):
        parts = []
        for i, ref in enumerate(q_refs):
            for g in range(GROUP):
                head = kv * GROUP + g
                q = ref[:, head * HEAD_DIM : (head + 1) * HEAD_DIM].astype(jnp.float32)
                parts.append(jnp.concatenate([q, last[i]], axis=1))
        q_all = jnp.concatenate(parts, axis=0).astype(jnp.bfloat16)
        scores = []
        for ref, hide in zip(k_refs, hides):
            k = ref[:, kv * HEAD_DIM : (kv + 1) * HEAD_DIM]
            scores.append(
                lax.dot_general(
                    q_all,
                    jnp.concatenate([k, hide], axis=1),
                    (((1,), (1,)), ((), ())),
                    preferred_element_type=jnp.float32,
                )
            )
        top = functools.reduce(
            jnp.maximum, [jnp.max(s, axis=1, keepdims=True) for s in scores]
        )
        top = top.astype(jnp.bfloat16).astype(jnp.float32)
        for j, s in enumerate(scores):
            weight_ref[
                kv * count : (kv + 1) * count, j * tokens : (j + 1) * tokens
            ] = jnp.exp2((s - top) * EXP2_SCALE).astype(jnp.bfloat16)
        for i in range(n_q):
            for g in range(GROUP):
                at = slice((i * GROUP + g) * rows, (i * GROUP + g + 1) * rows)
                tops[i] = jnp.where(lane == kv * GROUP + g, top[at], tops[i])
    for i in range(n_q):
        top_ref[i * rows : (i + 1) * rows, :] = tops[i]


def weighted(weight_ref, rows, refs, first, kv):
    tokens = refs[0].shape[0]
    ones = jnp.ones((tokens, LANES), jnp.bfloat16)
    parts = []
    for j, ref in enumerate(refs, first):
        v = jnp.concatenate(
            [ref[:, kv * HEAD_DIM : (kv + 1) * HEAD_DIM], ones], axis=1
        )
        weights = weight_ref[rows, j * tokens : (j + 1) * tokens]
        parts.append(jnp.dot(weights, v, preferred_element_type=jnp.float32))
    return functools.reduce(jnp.add, parts)


def early_kernel(weight_ref, *refs):
    v_refs, sum_ref = refs[:-1], refs[-1]
    count = weight_ref.shape[0] // KV_HEADS
    for kv in range(KV_HEADS):
        rows = slice(kv * count, (kv + 1) * count)
        sum_ref[rows, :] = weighted(weight_ref, rows, v_refs, 0, kv)


def late_kernel(n_q, weight_ref, top_ref, sum_ref, v_ref, *out_refs):
    rows, tokens = out_refs[0].shape[0], v_ref.shape[0]
    block = weight_ref.shape[1] // tokens - 1
    count = n_q * GROUP * rows
    lane = lax.broadcasted_iota(jnp.int32, (rows, LANES), 1)
    stats = [top_ref[i * rows : (i + 1) * rows, :] for i in range(n_q)]
    for kv in range(KV_HEADS):
        span = slice(kv * count, (kv + 1) * count)
        total = sum_ref[span, :] + weighted(weight_ref, span, [v_ref], block, kv)
        for i, ref in enumerate(out_refs):
            for g in range(GROUP):
                head = kv * GROUP + g
                at = slice((i * GROUP + g) * rows, (i * GROUP + g + 1) * rows)
                ref[:, head * HEAD_DIM : (head + 1) * HEAD_DIM] = total[
                    at, :HEAD_DIM
                ].astype(jnp.bfloat16)
                mass = total[at, HEAD_DIM:]
                high = mass.astype(jnp.bfloat16).astype(jnp.float32)
                stats[i] = jnp.where(lane == HEADS + head, high, stats[i])
                stats[i] = jnp.where(lane == 2 * HEADS + head, mass - high, stats[i])
    for stat, ref in zip(stats, out_refs):
        ref[:, WIDTH:] = stat.astype(jnp.bfloat16)


def weights_call(q_blocks, k_blocks, page_blocks):
    n_q, n_kv = len(q_blocks), len(k_blocks)
    rows, tokens = q_blocks[0].shape[0], k_blocks[0].shape[0]
    return pl.pallas_call(
        functools.partial(weights_kernel, n_q, n_kv),
        out_shape=[
            jax.ShapeDtypeStruct((n_q * HEADS * rows, n_kv * tokens), jnp.bfloat16),
            jax.ShapeDtypeStruct((n_q * rows, LANES), jnp.float32),
        ],
        in_specs=[VMEM_BLOCK] * (n_q + 2 * n_kv),
        out_specs=[VMEM_BLOCK] * 2,
        compiler_params=pltpu.CompilerParams(vmem_limit_bytes=24 << 20),
    )(*q_blocks, *k_blocks, *page_blocks)


def early_call(weights, v_blocks):
    return pl.pallas_call(
        early_kernel,
        out_shape=jax.ShapeDtypeStruct((weights.shape[0], 2 * LANES), jnp.float32),
        in_specs=[VMEM_BLOCK] * (1 + len(v_blocks)),
        out_specs=VMEM_BLOCK,
        compiler_params=pltpu.CompilerParams(vmem_limit_bytes=24 << 20),
    )(weights, *v_blocks)


def late_call(weights, tops, sums, v_block, n_q):
    rows = tops.shape[0] // n_q
    return pl.pallas_call(
        functools.partial(late_kernel, n_q),
        out_shape=[jax.ShapeDtypeStruct((rows, WIDTH + LANES), jnp.bfloat16)] * n_q,
        in_specs=[VMEM_BLOCK] * 4,
        out_specs=[VMEM_BLOCK] * n_q,
        compiler_params=pltpu.CompilerParams(vmem_limit_bytes=24 << 20),
    )(weights, tops, sums, v_block)


def merge_kernel(n, *refs):
    parts, out_ref = refs[:n], refs[n]
    tops, masses = [], []
    for ref in parts:
        stat = ref[:, WIDTH:].astype(jnp.float32)
        tops.append(stat)
        masses.append(
            pltpu.roll(stat, LANES - HEADS, 1) + pltpu.roll(stat, LANES - 2 * HEADS, 1)
        )
    top = functools.reduce(jnp.maximum, tops)
    factors = [jnp.exp2((t - top) * EXP2_SCALE) for t in tops]
    total = functools.reduce(jnp.add, [f * m for f, m in zip(factors, masses)])
    shares = [f / total for f in factors]
    for head in range(HEADS):
        at = slice(head * HEAD_DIM, (head + 1) * HEAD_DIM)
        value = functools.reduce(
            jnp.add,
            [
                share[:, head : head + 1] * ref[:, at].astype(jnp.float32)
                for share, ref in zip(shares, parts)
            ],
        )
        out_ref[:, at] = value.astype(jnp.bfloat16)


def merge_call(parts):
    rows = parts[0].shape[0]
    return pl.pallas_call(
        functools.partial(merge_kernel, len(parts)),
        out_shape=jax.ShapeDtypeStruct((rows, WIDTH), jnp.bfloat16),
        in_specs=[VMEM_BLOCK] * len(parts),
        out_specs=VMEM_BLOCK,
        compiler_params=pltpu.CompilerParams(vmem_limit_bytes=8 << 20),
    )(*parts)


def pooled(block, own):
    across = swapped(block, 2)
    beside = swapped(block, 1)
    return [own, beside, across, swapped(across, 1)]


def attend(queries, key_cache, value_cache, tile_page, row_last):
    groups = lax.axis_size("blk") // SHARE
    pages = tile_page.reshape(1, -1)
    own_q, own_k, own_v, own_page = stage_call(
        row_last, queries, key_cache, value_cache, pages
    )
    k_blocks = pooled(key_cache, own_k)
    v_blocks = pooled(value_cache, own_v)
    page_blocks = pooled(pages, own_page)
    q_blocks = [own_q] + [swapped(own_q, SHARE * d) for d in range(1, groups)]
    partials = []
    for start in range(0, groups, 4):
        some = q_blocks[start : start + 4]
        weights, tops = weights_call(some, k_blocks, page_blocks)
        sums = early_call(weights, v_blocks[:-1])
        partials += late_call(weights, tops, sums, v_blocks[-1], len(some))
    parts = [partials[0]] + [swapped(partials[d], SHARE * d) for d in range(1, groups)]
    return merge_call(parts)


def solution(mesh):
    placed = (
        P(("parts", "blk"), None),
        P(("parts", "blk"), None),
        P(("parts", "blk"), None),
        P(("parts", "blk")),
        P(("parts", "blk")),
    )
    return jax.shard_map(
        attend, mesh=mesh, in_specs=placed, out_specs=P(("parts", "blk"), None), check_vma=False
    )
```

```python
import functools
import math

import jax
import jax.numpy as jnp
from jax import lax
from jax.experimental import pallas as pl
from jax.experimental.pallas import tpu as pltpu
from jax.sharding import PartitionSpec as P


HEADS = 32
KV_HEADS = 4
GROUP = HEADS // KV_HEADS
HEAD_DIM = 128
WIDTH = HEADS * HEAD_DIM
LANES = 128
SHARE = 4
FAR = -(2.0**100)
EXP2_SCALE = math.log2(math.e) / math.sqrt(HEAD_DIM)


def swapped(block, distance):
    devices = lax.axis_size("blk")
    return lax.ppermute(block, "blk", [(i, i ^ distance) for i in range(devices)])


VMEM_BLOCK = pl.BlockSpec(memory_space=pltpu.VMEM)


HBM_BLOCK = pl.BlockSpec(memory_space=pltpu.MemorySpace.HBM)


def in_hbm(array):
    return pltpu.with_memory_space_constraint(array, pltpu.MemorySpace.HBM)


def limits_kernel(q_ref, last_ref, q_out, last, sems):
    rows = q_ref.shape[0]
    moves = ((last_ref, last), (q_ref, q_out.at[:, :WIDTH]))
    copies = [pltpu.make_async_copy(s, d, sems.at[i]) for i, (s, d) in enumerate(moves)]
    for copy in copies:
        copy.start()
    row = lax.broadcasted_iota(jnp.int32, (rows, LANES), 0)
    lane = lax.broadcasted_iota(jnp.int32, (rows, LANES), 1)
    copies[0].wait()
    seen = functools.reduce(
        jnp.logical_or, [(row == r) & (lane == last[r]) for r in range(rows)]
    )
    q_out[:, WIDTH:] = jnp.where(seen, 1.0, 0.0).astype(jnp.bfloat16)
    copies[1].wait()


def limits_call(queries, row_last):
    rows = queries.shape[0]
    return pl.pallas_call(
        limits_kernel,
        out_shape=jax.ShapeDtypeStruct((rows, WIDTH + LANES), jnp.bfloat16),
        in_specs=[HBM_BLOCK] * 2,
        out_specs=VMEM_BLOCK,
        scratch_shapes=[pltpu.SMEM((rows,), jnp.int32), pltpu.SemaphoreType.DMA((2,))],
        compiler_params=pltpu.CompilerParams(vmem_limit_bytes=8 << 20),
    )(in_hbm(queries), in_hbm(row_last))


def stage_kernel(*refs):
    sources, targets, sems = refs[: len(refs) // 2], refs[len(refs) // 2 : -1], refs[-1]
    copies = [
        pltpu.make_async_copy(source, target, sems.at[i])
        for i, (source, target) in enumerate(zip(sources, targets))
    ]
    for copy in copies:
        copy.start()
    for copy in copies:
        copy.wait()


def stage_call(*arrays):
    return pl.pallas_call(
        stage_kernel,
        out_shape=[jax.ShapeDtypeStruct(a.shape, a.dtype) for a in arrays],
        in_specs=[HBM_BLOCK] * len(arrays),
        out_specs=[VMEM_BLOCK] * len(arrays),
        scratch_shapes=[pltpu.SemaphoreType.DMA((len(arrays),))],
        compiler_params=pltpu.CompilerParams(vmem_limit_bytes=8 << 20),
    )(*map(in_hbm, arrays))


def weights_kernel(n_q, n_kv, *refs):
    q_refs, k_refs = refs[:n_q], refs[n_q : n_q + n_kv]
    page_refs = refs[n_q + n_kv : n_q + 2 * n_kv]
    weight_ref, top_ref = refs[n_q + 2 * n_kv :]
    rows, tokens = q_refs[0].shape[0], k_refs[0].shape[0]
    lane = lax.broadcasted_iota(jnp.int32, (rows, LANES), 1)
    token_lane = lax.broadcasted_iota(jnp.int32, (tokens, LANES), 1).astype(jnp.float32)
    pick = jnp.where(
        lax.broadcasted_iota(jnp.int32, (8, LANES), 0) == 0, 1.0, 0.0
    ).astype(jnp.bfloat16)
    hides = []
    for ref in page_refs:
        pages = jnp.broadcast_to(ref[...], (8, tokens)).astype(jnp.float32)
        column = lax.dot_general(
            pages.astype(jnp.bfloat16),
            pick,
            (((0,), (0,)), ((), ())),
            preferred_element_type=jnp.float32,
        )
        hides.append(jnp.where(column > token_lane, FAR, 0.0).astype(jnp.bfloat16))
    tops = [jnp.zeros((rows, LANES), jnp.float32)] * n_q
    last = [ref[:, WIDTH:].astype(jnp.float32) for ref in q_refs]
    count = n_q * GROUP * rows
    for kv in range(KV_HEADS):
        parts = []
        for i, ref in enumerate(q_refs):
            for g in range(GROUP):
                head = kv * GROUP + g
                q = ref[:, head * HEAD_DIM : (head + 1) * HEAD_DIM].astype(jnp.float32)
                parts.append(jnp.concatenate([q, last[i]], axis=1))
        q_all = jnp.concatenate(parts, axis=0).astype(jnp.bfloat16)
        scores = []
        for ref, hide in zip(k_refs, hides):
            k = ref[:, kv * HEAD_DIM : (kv + 1) * HEAD_DIM]
            scores.append(
                lax.dot_general(
                    q_all,
                    jnp.concatenate([k, hide], axis=1),
                    (((1,), (1,)), ((), ())),
                    preferred_element_type=jnp.float32,
                )
            )
        top = functools.reduce(
            jnp.maximum, [jnp.max(s, axis=1, keepdims=True) for s in scores]
        )
        top = top.astype(jnp.bfloat16).astype(jnp.float32)
        for j, s in enumerate(scores):
            weight_ref[
                kv * count : (kv + 1) * count, j * tokens : (j + 1) * tokens
            ] = jnp.exp2((s - top) * EXP2_SCALE).astype(jnp.bfloat16)
        for i in range(n_q):
            for g in range(GROUP):
                at = slice((i * GROUP + g) * rows, (i * GROUP + g + 1) * rows)
                tops[i] = jnp.where(lane == kv * GROUP + g, top[at], tops[i])
    for i in range(n_q):
        top_ref[i * rows : (i + 1) * rows, :] = tops[i]


def weighted(weight_ref, rows, refs, first, kv):
    tokens = refs[0].shape[0]
    ones = jnp.ones((tokens, LANES), jnp.bfloat16)
    parts = []
    for j, ref in enumerate(refs, first):
        v = jnp.concatenate(
            [ref[:, kv * HEAD_DIM : (kv + 1) * HEAD_DIM], ones], axis=1
        )
        weights = weight_ref[rows, j * tokens : (j + 1) * tokens]
        parts.append(jnp.dot(weights, v, preferred_element_type=jnp.float32))
    return functools.reduce(jnp.add, parts)


def early_kernel(weight_ref, *refs):
    v_refs, sum_ref = refs[:-1], refs[-1]
    count = weight_ref.shape[0] // KV_HEADS
    for kv in range(KV_HEADS):
        rows = slice(kv * count, (kv + 1) * count)
        sum_ref[rows, :] = weighted(weight_ref, rows, v_refs, 0, kv)


def late_kernel(n_q, weight_ref, top_ref, sum_ref, v_ref, *out_refs):
    rows, tokens = out_refs[0].shape[0], v_ref.shape[0]
    block = weight_ref.shape[1] // tokens - 1
    count = n_q * GROUP * rows
    lane = lax.broadcasted_iota(jnp.int32, (rows, LANES), 1)
    stats = [top_ref[i * rows : (i + 1) * rows, :] for i in range(n_q)]
    for kv in range(KV_HEADS):
        span = slice(kv * count, (kv + 1) * count)
        total = sum_ref[span, :] + weighted(weight_ref, span, [v_ref], block, kv)
        for i, ref in enumerate(out_refs):
            for g in range(GROUP):
                head = kv * GROUP + g
                at = slice((i * GROUP + g) * rows, (i * GROUP + g + 1) * rows)
                ref[:, head * HEAD_DIM : (head + 1) * HEAD_DIM] = total[
                    at, :HEAD_DIM
                ].astype(jnp.bfloat16)
                mass = total[at, HEAD_DIM:]
                high = mass.astype(jnp.bfloat16).astype(jnp.float32)
                stats[i] = jnp.where(lane == HEADS + head, high, stats[i])
                stats[i] = jnp.where(lane == 2 * HEADS + head, mass - high, stats[i])
    for stat, ref in zip(stats, out_refs):
        ref[:, WIDTH:] = stat.astype(jnp.bfloat16)


def weights_call(q_blocks, k_blocks, page_blocks):
    n_q, n_kv = len(q_blocks), len(k_blocks)
    rows, tokens = q_blocks[0].shape[0], k_blocks[0].shape[0]
    return pl.pallas_call(
        functools.partial(weights_kernel, n_q, n_kv),
        out_shape=[
            jax.ShapeDtypeStruct((n_q * HEADS * rows, n_kv * tokens), jnp.bfloat16),
            jax.ShapeDtypeStruct((n_q * rows, LANES), jnp.float32),
        ],
        in_specs=[VMEM_BLOCK] * (n_q + 2 * n_kv),
        out_specs=[VMEM_BLOCK] * 2,
        compiler_params=pltpu.CompilerParams(vmem_limit_bytes=24 << 20),
    )(*q_blocks, *k_blocks, *page_blocks)


def early_call(weights, v_blocks):
    return pl.pallas_call(
        early_kernel,
        out_shape=jax.ShapeDtypeStruct((weights.shape[0], 2 * LANES), jnp.float32),
        in_specs=[VMEM_BLOCK] * (1 + len(v_blocks)),
        out_specs=VMEM_BLOCK,
        compiler_params=pltpu.CompilerParams(vmem_limit_bytes=24 << 20),
    )(weights, *v_blocks)


def late_call(weights, tops, sums, v_block, n_q):
    rows = tops.shape[0] // n_q
    return pl.pallas_call(
        functools.partial(late_kernel, n_q),
        out_shape=[jax.ShapeDtypeStruct((rows, WIDTH + LANES), jnp.bfloat16)] * n_q,
        in_specs=[VMEM_BLOCK] * 4,
        out_specs=[VMEM_BLOCK] * n_q,
        compiler_params=pltpu.CompilerParams(vmem_limit_bytes=24 << 20),
    )(weights, tops, sums, v_block)


def stats_of(ref):
    stat = ref[:, WIDTH:].astype(jnp.float32)
    mass = pltpu.roll(stat, LANES - HEADS, 1) + pltpu.roll(stat, LANES - 2 * HEADS, 1)
    return stat, mass


def join_kernel(n, *refs):
    parts, sum_ref, stat_ref = refs[:n], refs[n], refs[n + 1]
    tops, masses = zip(*map(stats_of, parts))
    top = functools.reduce(jnp.maximum, tops)
    factors = [jnp.exp2((t - top) * EXP2_SCALE) for t in tops]
    stat_ref[:, :LANES] = top
    stat_ref[:, LANES:] = functools.reduce(
        jnp.add, [f * m for f, m in zip(factors, masses)]
    )
    for head in range(HEADS):
        at = slice(head * HEAD_DIM, (head + 1) * HEAD_DIM)
        sum_ref[:, at] = functools.reduce(
            jnp.add,
            [
                factor[:, head : head + 1] * ref[:, at].astype(jnp.float32)
                for factor, ref in zip(factors, parts)
            ],
        )


def merge_kernel(sum_ref, stat_ref, part_ref, out_ref):
    top, mass = stat_ref[:, :LANES], stat_ref[:, LANES:]
    part_top, part_mass = stats_of(part_ref)
    best = jnp.maximum(top, part_top)
    factor = jnp.exp2((top - best) * EXP2_SCALE)
    part_factor = jnp.exp2((part_top - best) * EXP2_SCALE)
    total = factor * mass + part_factor * part_mass
    share, part_share = factor / total, part_factor / total
    for head in range(HEADS):
        at = slice(head * HEAD_DIM, (head + 1) * HEAD_DIM)
        part = part_ref[:, at].astype(jnp.float32)
        value = share[:, head : head + 1] * sum_ref[:, at]
        value = value + part_share[:, head : head + 1] * part
        out_ref[:, at] = value.astype(jnp.bfloat16)


def join_call(parts):
    rows = parts[0].shape[0]
    return pl.pallas_call(
        functools.partial(join_kernel, len(parts)),
        out_shape=[
            jax.ShapeDtypeStruct((rows, WIDTH), jnp.float32),
            jax.ShapeDtypeStruct((rows, 2 * LANES), jnp.float32),
        ],
        in_specs=[VMEM_BLOCK] * len(parts),
        out_specs=[VMEM_BLOCK] * 2,
        compiler_params=pltpu.CompilerParams(vmem_limit_bytes=8 << 20),
    )(*parts)


def merge_call(sums, stats, part):
    return pl.pallas_call(
        merge_kernel,
        out_shape=jax.ShapeDtypeStruct(sums.shape, jnp.bfloat16),
        in_specs=[VMEM_BLOCK] * 3,
        out_specs=VMEM_BLOCK,
        compiler_params=pltpu.CompilerParams(vmem_limit_bytes=8 << 20),
    )(sums, stats, part)


def pooled(block, own):
    across = swapped(block, 2)
    beside = swapped(block, 1)
    return [own, beside, across, swapped(across, 1)]


def attend(queries, key_cache, value_cache, tile_page, row_last):
    groups = lax.axis_size("blk") // SHARE
    pages = tile_page.reshape(1, -1)
    own_q = limits_call(queries, row_last)
    own_k, own_v, own_page = stage_call(key_cache, value_cache, pages)
    k_blocks = pooled(key_cache, own_k)
    v_blocks = pooled(value_cache, own_v)
    page_blocks = pooled(pages, own_page)
    q_blocks = [own_q] + [swapped(own_q, SHARE * d) for d in range(1, groups)]
    partials = []
    for start in range(0, groups, 4):
        some = q_blocks[start : start + 4]
        weights, tops = weights_call(some, k_blocks, page_blocks)
        sums = early_call(weights, v_blocks[:-1])
        partials += late_call(weights, tops, sums, v_blocks[-1], len(some))
    parts = [partials[0]] + [swapped(partials[d], SHARE * d) for d in range(1, groups)]
    sums, stats = join_call(parts[:2] + parts[3:])
    return merge_call(sums, stats, parts[2])


def solution(mesh):
    placed = (
        P(("parts", "blk"), None),
        P(("parts", "blk"), None),
        P(("parts", "blk"), None),
        P(("parts", "blk")),
        P(("parts", "blk")),
    )
    return jax.shard_map(
        attend, mesh=mesh, in_specs=placed, out_specs=P(("parts", "blk"), None), check_vma=False
    )
```

```python
import functools
import math

import jax
import jax.numpy as jnp
from jax import lax
from jax.experimental import pallas as pl
from jax.experimental.pallas import tpu as pltpu
from jax.sharding import PartitionSpec as P


HEADS = 32
KV_HEADS = 4
GROUP = HEADS // KV_HEADS
HEAD_DIM = 128
WIDTH = HEADS * HEAD_DIM
LANES = 128
SHARE = 4
FAR = -(2.0**100)
EXP2_SCALE = math.log2(math.e) / math.sqrt(HEAD_DIM)


def swapped(block, distance):
    devices = lax.axis_size("blk")
    return lax.ppermute(block, "blk", [(i, i ^ distance) for i in range(devices)])


VMEM_BLOCK = pl.BlockSpec(memory_space=pltpu.VMEM)


HBM_BLOCK = pl.BlockSpec(memory_space=pltpu.MemorySpace.HBM)


def in_hbm(array):
    return pltpu.with_memory_space_constraint(array, pltpu.MemorySpace.HBM)


def stage_kernel(
    q_ref, k_ref, v_ref, page_ref, last_ref, q_out, k_out, v_out, page, last, sems
):
    rows, tokens = q_ref.shape[0], k_ref.shape[0]
    moves = (
        (last_ref, last),
        (q_ref, q_out.at[:, :WIDTH]),
        (page_ref, page),
        (k_ref, k_out.at[:tokens, :]),
        (v_ref, v_out),
    )
    copies = [pltpu.make_async_copy(s, d, sems.at[i]) for i, (s, d) in enumerate(moves)]
    for copy in copies:
        copy.start()
    row = lax.broadcasted_iota(jnp.int32, (rows, LANES), 0)
    lane = lax.broadcasted_iota(jnp.int32, (rows, LANES), 1)
    copies[0].wait()
    seen = functools.reduce(
        jnp.logical_or, [(row == r) & (lane == last[r]) for r in range(rows)]
    )
    q_out[:, WIDTH:] = jnp.where(seen, 1.0, 0.0).astype(jnp.bfloat16)
    for copy in copies[1:]:
        copy.wait()
    filled = jnp.broadcast_to(page[...], (8, tokens)).astype(jnp.float32)
    k_out[tokens:, :tokens] = filled.astype(jnp.bfloat16)
    k_out[tokens:, tokens:] = jnp.zeros((8, k_out.shape[1] - tokens), jnp.bfloat16)


def stage_call(row_last, queries, key_cache, value_cache, pages):
    rows, (tokens, width) = queries.shape[0], key_cache.shape
    return pl.pallas_call(
        stage_kernel,
        out_shape=[
            jax.ShapeDtypeStruct((rows, WIDTH + LANES), jnp.bfloat16),
            jax.ShapeDtypeStruct((tokens + 8, width), jnp.bfloat16),
            jax.ShapeDtypeStruct(value_cache.shape, jnp.bfloat16),
        ],
        in_specs=[HBM_BLOCK] * 5,
        out_specs=[VMEM_BLOCK] * 3,
        scratch_shapes=[
            pltpu.VMEM(pages.shape, jnp.int32),
            pltpu.SMEM((rows,), jnp.int32),
            pltpu.SemaphoreType.DMA((5,)),
        ],
        compiler_params=pltpu.CompilerParams(vmem_limit_bytes=8 << 20),
    )(*map(in_hbm, (queries, key_cache, value_cache, pages, row_last)))


def weights_kernel(n_q, n_kv, *refs):
    q_refs, k_refs = refs[:n_q], refs[n_q : n_q + n_kv]
    page_refs = refs[n_q + n_kv : n_q + n_kv + 2]
    weight_ref, top_ref = refs[n_q + n_kv + 2 :]
    rows, tokens = q_refs[0].shape[0], k_refs[-1].shape[0]
    lane = lax.broadcasted_iota(jnp.int32, (rows, LANES), 1)
    token_lane = lax.broadcasted_iota(jnp.int32, (tokens, LANES), 1).astype(jnp.float32)
    pick = jnp.where(
        lax.broadcasted_iota(jnp.int32, (8, LANES), 0) == 0, 1.0, 0.0
    ).astype(jnp.bfloat16)
    hides = []
    page_rows = [ref[tokens:, :tokens] for ref in k_refs[:2]]
    for ref in page_refs:
        pages = jnp.broadcast_to(ref[...], (8, tokens)).astype(jnp.float32)
        page_rows.append(pages.astype(jnp.bfloat16))
    for pages in page_rows:
        column = lax.dot_general(
            pages, pick, (((0,), (0,)), ((), ())), preferred_element_type=jnp.float32
        )
        hides.append(jnp.where(column > token_lane, FAR, 0.0).astype(jnp.bfloat16))
    tops = [jnp.zeros((rows, LANES), jnp.float32)] * n_q
    last = [ref[:, WIDTH:].astype(jnp.float32) for ref in q_refs]
    count = n_q * GROUP * rows
    for kv in range(KV_HEADS):
        parts = []
        for i, ref in enumerate(q_refs):
            for g in range(GROUP):
                head = kv * GROUP + g
                q = ref[:, head * HEAD_DIM : (head + 1) * HEAD_DIM].astype(jnp.float32)
                parts.append(jnp.concatenate([q, last[i]], axis=1))
        q_all = jnp.concatenate(parts, axis=0).astype(jnp.bfloat16)
        scores = []
        for ref, hide in zip(k_refs, hides):
            k = ref[:tokens, kv * HEAD_DIM : (kv + 1) * HEAD_DIM]
            scores.append(
                lax.dot_general(
                    q_all,
                    jnp.concatenate([k, hide], axis=1),
                    (((1,), (1,)), ((), ())),
                    preferred_element_type=jnp.float32,
                )
            )
        top = functools.reduce(
            jnp.maximum, [jnp.max(s, axis=1, keepdims=True) for s in scores]
        )
        top = top.astype(jnp.bfloat16).astype(jnp.float32)
        for j, s in enumerate(scores):
            weight_ref[
                kv * count : (kv + 1) * count, j * tokens : (j + 1) * tokens
            ] = jnp.exp2((s - top) * EXP2_SCALE).astype(jnp.bfloat16)
        for i in range(n_q):
            for g in range(GROUP):
                at = slice((i * GROUP + g) * rows, (i * GROUP + g + 1) * rows)
                tops[i] = jnp.where(lane == kv * GROUP + g, top[at], tops[i])
    for i in range(n_q):
        top_ref[i * rows : (i + 1) * rows, :] = tops[i]


def weighted(weight_ref, rows, refs, first, kv):
    tokens = refs[0].shape[0]
    ones = jnp.ones((tokens, LANES), jnp.bfloat16)
    parts = []
    for j, ref in enumerate(refs, first):
        v = jnp.concatenate(
            [ref[:, kv * HEAD_DIM : (kv + 1) * HEAD_DIM], ones], axis=1
        )
        weights = weight_ref[rows, j * tokens : (j + 1) * tokens]
        parts.append(jnp.dot(weights, v, preferred_element_type=jnp.float32))
    return functools.reduce(jnp.add, parts)


def early_kernel(weight_ref, *refs):
    v_refs, sum_ref = refs[:-1], refs[-1]
    count = weight_ref.shape[0] // KV_HEADS
    for kv in range(KV_HEADS):
        rows = slice(kv * count, (kv + 1) * count)
        sum_ref[rows, :] = weighted(weight_ref, rows, v_refs, 0, kv)


def late_kernel(n_q, weight_ref, top_ref, sum_ref, v_ref, *out_refs):
    rows, tokens = out_refs[0].shape[0], v_ref.shape[0]
    block = weight_ref.shape[1] // tokens - 1
    count = n_q * GROUP * rows
    lane = lax.broadcasted_iota(jnp.int32, (rows, LANES), 1)
    stats = [top_ref[i * rows : (i + 1) * rows, :] for i in range(n_q)]
    for kv in range(KV_HEADS):
        span = slice(kv * count, (kv + 1) * count)
        total = sum_ref[span, :] + weighted(weight_ref, span, [v_ref], block, kv)
        for i, ref in enumerate(out_refs):
            for g in range(GROUP):
                head = kv * GROUP + g
                at = slice((i * GROUP + g) * rows, (i * GROUP + g + 1) * rows)
                ref[:, head * HEAD_DIM : (head + 1) * HEAD_DIM] = total[
                    at, :HEAD_DIM
                ].astype(jnp.bfloat16)
                mass = total[at, HEAD_DIM:]
                high = mass.astype(jnp.bfloat16).astype(jnp.float32)
                stats[i] = jnp.where(lane == HEADS + head, high, stats[i])
                stats[i] = jnp.where(lane == 2 * HEADS + head, mass - high, stats[i])
    for stat, ref in zip(stats, out_refs):
        ref[:, WIDTH:] = stat.astype(jnp.bfloat16)


def weights_call(q_blocks, k_blocks, page_blocks):
    n_q, n_kv = len(q_blocks), len(k_blocks)
    rows, tokens = q_blocks[0].shape[0], k_blocks[-1].shape[0]
    return pl.pallas_call(
        functools.partial(weights_kernel, n_q, n_kv),
        out_shape=[
            jax.ShapeDtypeStruct((n_q * HEADS * rows, n_kv * tokens), jnp.bfloat16),
            jax.ShapeDtypeStruct((n_q * rows, LANES), jnp.float32),
        ],
        in_specs=[VMEM_BLOCK] * (n_q + n_kv + 2),
        out_specs=[VMEM_BLOCK] * 2,
        compiler_params=pltpu.CompilerParams(vmem_limit_bytes=24 << 20),
    )(*q_blocks, *k_blocks, *page_blocks)


def early_call(weights, v_blocks):
    return pl.pallas_call(
        early_kernel,
        out_shape=jax.ShapeDtypeStruct((weights.shape[0], 2 * LANES), jnp.float32),
        in_specs=[VMEM_BLOCK] * (1 + len(v_blocks)),
        out_specs=VMEM_BLOCK,
        compiler_params=pltpu.CompilerParams(vmem_limit_bytes=24 << 20),
    )(weights, *v_blocks)


def late_call(weights, tops, sums, v_block, n_q):
    rows = tops.shape[0] // n_q
    return pl.pallas_call(
        functools.partial(late_kernel, n_q),
        out_shape=[jax.ShapeDtypeStruct((rows, WIDTH + LANES), jnp.bfloat16)] * n_q,
        in_specs=[VMEM_BLOCK] * 4,
        out_specs=[VMEM_BLOCK] * n_q,
        compiler_params=pltpu.CompilerParams(vmem_limit_bytes=24 << 20),
    )(weights, tops, sums, v_block)


def stats_of(ref):
    stat = ref[:, WIDTH:].astype(jnp.float32)
    mass = pltpu.roll(stat, LANES - HEADS, 1) + pltpu.roll(stat, LANES - 2 * HEADS, 1)
    return stat, mass


def join_kernel(n, *refs):
    parts, sum_ref, stat_ref = refs[:n], refs[n], refs[n + 1]
    tops, masses = zip(*map(stats_of, parts))
    top = functools.reduce(jnp.maximum, tops)
    factors = [jnp.exp2((t - top) * EXP2_SCALE) for t in tops]
    stat_ref[:, :LANES] = top
    stat_ref[:, LANES:] = functools.reduce(
        jnp.add, [f * m for f, m in zip(factors, masses)]
    )
    for head in range(HEADS):
        at = slice(head * HEAD_DIM, (head + 1) * HEAD_DIM)
        sum_ref[:, at] = functools.reduce(
            jnp.add,
            [
                factor[:, head : head + 1] * ref[:, at].astype(jnp.float32)
                for factor, ref in zip(factors, parts)
            ],
        )


def merge_kernel(sum_ref, stat_ref, part_ref, out_ref):
    top, mass = stat_ref[:, :LANES], stat_ref[:, LANES:]
    part_top, part_mass = stats_of(part_ref)
    best = jnp.maximum(top, part_top)
    factor = jnp.exp2((top - best) * EXP2_SCALE)
    part_factor = jnp.exp2((part_top - best) * EXP2_SCALE)
    total = factor * mass + part_factor * part_mass
    share, part_share = factor / total, part_factor / total
    for head in range(HEADS):
        at = slice(head * HEAD_DIM, (head + 1) * HEAD_DIM)
        part = part_ref[:, at].astype(jnp.float32)
        value = share[:, head : head + 1] * sum_ref[:, at]
        value = value + part_share[:, head : head + 1] * part
        out_ref[:, at] = value.astype(jnp.bfloat16)


def join_call(parts):
    rows = parts[0].shape[0]
    return pl.pallas_call(
        functools.partial(join_kernel, len(parts)),
        out_shape=[
            jax.ShapeDtypeStruct((rows, WIDTH), jnp.float32),
            jax.ShapeDtypeStruct((rows, 2 * LANES), jnp.float32),
        ],
        in_specs=[VMEM_BLOCK] * len(parts),
        out_specs=[VMEM_BLOCK] * 2,
        compiler_params=pltpu.CompilerParams(vmem_limit_bytes=8 << 20),
    )(*parts)


def merge_call(sums, stats, part):
    return pl.pallas_call(
        merge_kernel,
        out_shape=jax.ShapeDtypeStruct(sums.shape, jnp.bfloat16),
        in_specs=[VMEM_BLOCK] * 3,
        out_specs=VMEM_BLOCK,
        compiler_params=pltpu.CompilerParams(vmem_limit_bytes=8 << 20),
    )(sums, stats, part)


def pooled(block, own):
    across = swapped(block, 2)
    beside = swapped(block, 1)
    return [own, beside, across, swapped(across, 1)]


def attend(queries, key_cache, value_cache, tile_page, row_last):
    groups = lax.axis_size("blk") // SHARE
    pages = tile_page.reshape(1, -1)
    own_q, own_k, own_v = stage_call(row_last, queries, key_cache, value_cache, pages)
    across = swapped(key_cache, 2)
    k_blocks = [own_k, swapped(own_k, 1), across]
    k_blocks.append(swapped(across, 1))
    v_blocks = pooled(value_cache, own_v)
    across = swapped(pages, 2)
    page_blocks = [across, swapped(across, 1)]
    q_blocks = [own_q] + [swapped(own_q, SHARE * d) for d in range(1, groups)]
    partials = []
    for start in range(0, groups, 4):
        some = q_blocks[start : start + 4]
        weights, tops = weights_call(some, k_blocks, page_blocks)
        sums = early_call(weights, v_blocks[:-1])
        partials += late_call(weights, tops, sums, v_blocks[-1], len(some))
    parts = [partials[0]] + [swapped(partials[d], SHARE * d) for d in range(1, groups)]
    sums, stats = join_call(parts[:2] + parts[3:])
    return merge_call(sums, stats, parts[2])


def solution(mesh):
    placed = (
        P(("parts", "blk"), None),
        P(("parts", "blk"), None),
        P(("parts", "blk"), None),
        P(("parts", "blk")),
        P(("parts", "blk")),
    )
    return jax.shard_map(
        attend, mesh=mesh, in_specs=placed, out_specs=P(("parts", "blk"), None), check_vma=False
    )
```

```python
import functools
import math

import jax
import jax.numpy as jnp
from jax import lax
from jax.experimental import pallas as pl
from jax.experimental.pallas import tpu as pltpu
from jax.sharding import PartitionSpec as P


HEADS = 32
KV_HEADS = 4
GROUP = HEADS // KV_HEADS
HEAD_DIM = 128
WIDTH = HEADS * HEAD_DIM
LANES = 128
SHARE = 4
FAR = -(2.0**100)
EXP2_SCALE = math.log2(math.e) / math.sqrt(HEAD_DIM)


def swapped(block, distance):
    devices = lax.axis_size("blk")
    return lax.ppermute(block, "blk", [(i, i ^ distance) for i in range(devices)])


VMEM_BLOCK = pl.BlockSpec(memory_space=pltpu.VMEM)


HBM_BLOCK = pl.BlockSpec(memory_space=pltpu.MemorySpace.HBM)


def in_hbm(array):
    return pltpu.with_memory_space_constraint(array, pltpu.MemorySpace.HBM)


def stage_kernel(
    q_ref, k_ref, v_ref, page_ref, last_ref, q_out, k_out, v_out, page_out, last, sems
):
    rows = q_ref.shape[0]
    moves = (
        (last_ref, last),
        (q_ref, q_out.at[:, :WIDTH]),
        (page_ref, page_out),
        (k_ref, k_out),
        (v_ref, v_out),
    )
    copies = [pltpu.make_async_copy(s, d, sems.at[i]) for i, (s, d) in enumerate(moves)]
    for copy in copies:
        copy.start()
    row = lax.broadcasted_iota(jnp.int32, (rows, LANES), 0)
    lane = lax.broadcasted_iota(jnp.int32, (rows, LANES), 1)
    copies[0].wait()
    seen = functools.reduce(
        jnp.logical_or, [(row == r) & (lane == last[r]) for r in range(rows)]
    )
    q_out[:, WIDTH:] = jnp.where(seen, 1.0, 0.0).astype(jnp.bfloat16)
    for copy in copies[1:]:
        copy.wait()


def stage_call(row_last, queries, key_cache, value_cache, pages):
    rows = queries.shape[0]
    return pl.pallas_call(
        stage_kernel,
        out_shape=[
            jax.ShapeDtypeStruct((rows, WIDTH + LANES), jnp.bfloat16),
            jax.ShapeDtypeStruct(key_cache.shape, jnp.bfloat16),
            jax.ShapeDtypeStruct(value_cache.shape, jnp.bfloat16),
            jax.ShapeDtypeStruct(pages.shape, jnp.int32),
        ],
        in_specs=[HBM_BLOCK] * 5,
        out_specs=[VMEM_BLOCK] * 4,
        scratch_shapes=[pltpu.SMEM((rows,), jnp.int32), pltpu.SemaphoreType.DMA((5,))],
        compiler_params=pltpu.CompilerParams(vmem_limit_bytes=8 << 20),
    )(*map(in_hbm, (queries, key_cache, value_cache, pages, row_last)))


def weights_kernel(n_q, n_kv, *refs):
    q_refs, k_refs = refs[:n_q], refs[n_q : n_q + n_kv]
    page_refs = refs[n_q + n_kv : n_q + 2 * n_kv]
    weight_ref, top_ref = refs[n_q + 2 * n_kv :]
    rows, tokens = q_refs[0].shape[0], k_refs[0].shape[0]
    lane = lax.broadcasted_iota(jnp.int32, (rows, LANES), 1)
    token_lane = lax.broadcasted_iota(jnp.int32, (tokens, LANES), 1).astype(jnp.float32)
    pick = jnp.where(
        lax.broadcasted_iota(jnp.int32, (8, LANES), 0) == 0, 1.0, 0.0
    ).astype(jnp.bfloat16)
    hides = []
    for ref in page_refs:
        pages = jnp.broadcast_to(ref[...], (8, tokens)).astype(jnp.float32)
        column = lax.dot_general(
            pages.astype(jnp.bfloat16),
            pick,
            (((0,), (0,)), ((), ())),
            preferred_element_type=jnp.float32,
        )
        hides.append(jnp.where(column > token_lane, FAR, 0.0).astype(jnp.bfloat16))
    tops = [jnp.zeros((rows, LANES), jnp.float32)] * n_q
    last = [ref[:, WIDTH:].astype(jnp.float32) for ref in q_refs]
    count = n_q * GROUP * rows
    for kv in range(KV_HEADS):
        parts = []
        for i, ref in enumerate(q_refs):
            for g in range(GROUP):
                head = kv * GROUP + g
                q = ref[:, head * HEAD_DIM : (head + 1) * HEAD_DIM].astype(jnp.float32)
                parts.append(jnp.concatenate([q, last[i]], axis=1))
        q_all = jnp.concatenate(parts, axis=0).astype(jnp.bfloat16)
        scores = []
        for ref, hide in zip(k_refs, hides):
            k = ref[:, kv * HEAD_DIM : (kv + 1) * HEAD_DIM]
            scores.append(
                lax.dot_general(
                    q_all,
                    jnp.concatenate([k, hide], axis=1),
                    (((1,), (1,)), ((), ())),
                    preferred_element_type=jnp.float32,
                )
            )
        top = functools.reduce(
            jnp.maximum, [jnp.max(s, axis=1, keepdims=True) for s in scores]
        )
        top = top.astype(jnp.bfloat16).astype(jnp.float32)
        for j, s in enumerate(scores):
            weight_ref[
                kv * count : (kv + 1) * count, j * tokens : (j + 1) * tokens
            ] = jnp.exp2((s - top) * EXP2_SCALE).astype(jnp.bfloat16)
        for i in range(n_q):
            for g in range(GROUP):
                at = slice((i * GROUP + g) * rows, (i * GROUP + g + 1) * rows)
                tops[i] = jnp.where(lane == kv * GROUP + g, top[at], tops[i])
    for i in range(n_q):
        top_ref[i * rows : (i + 1) * rows, :] = tops[i]


def weighted(weight_ref, rows, refs, first, kv):
    tokens = refs[0].shape[0]
    ones = jnp.ones((tokens, LANES), jnp.bfloat16)
    parts = []
    for j, ref in enumerate(refs, first):
        v = jnp.concatenate(
            [ref[:, kv * HEAD_DIM : (kv + 1) * HEAD_DIM], ones], axis=1
        )
        weights = weight_ref[rows, j * tokens : (j + 1) * tokens]
        parts.append(jnp.dot(weights, v, preferred_element_type=jnp.float32))
    return functools.reduce(jnp.add, parts)


def early_kernel(weight_ref, *refs):
    v_refs, sum_ref = refs[:-1], refs[-1]
    count = weight_ref.shape[0] // KV_HEADS
    for kv in range(KV_HEADS):
        rows = slice(kv * count, (kv + 1) * count)
        sum_ref[rows, :] = weighted(weight_ref, rows, v_refs, 0, kv)


def late_kernel(n_q, weight_ref, top_ref, sum_ref, v_ref, *out_refs):
    rows, tokens = out_refs[0].shape[0], v_ref.shape[0]
    block = weight_ref.shape[1] // tokens - 1
    count = n_q * GROUP * rows
    lane = lax.broadcasted_iota(jnp.int32, (rows, LANES), 1)
    stats = [top_ref[i * rows : (i + 1) * rows, :] for i in range(n_q)]
    for kv in range(KV_HEADS):
        span = slice(kv * count, (kv + 1) * count)
        total = sum_ref[span, :] + weighted(weight_ref, span, [v_ref], block, kv)
        for i, ref in enumerate(out_refs):
            for g in range(GROUP):
                head = kv * GROUP + g
                at = slice((i * GROUP + g) * rows, (i * GROUP + g + 1) * rows)
                ref[:, head * HEAD_DIM : (head + 1) * HEAD_DIM] = total[
                    at, :HEAD_DIM
                ].astype(jnp.bfloat16)
                mass = total[at, HEAD_DIM:]
                high = mass.astype(jnp.bfloat16).astype(jnp.float32)
                stats[i] = jnp.where(lane == HEADS + head, high, stats[i])
                stats[i] = jnp.where(lane == 2 * HEADS + head, mass - high, stats[i])
    for stat, ref in zip(stats, out_refs):
        ref[:, WIDTH:] = stat.astype(jnp.bfloat16)


def weights_call(q_blocks, k_blocks, page_blocks):
    n_q, n_kv = len(q_blocks), len(k_blocks)
    rows, tokens = q_blocks[0].shape[0], k_blocks[0].shape[0]
    return pl.pallas_call(
        functools.partial(weights_kernel, n_q, n_kv),
        out_shape=[
            jax.ShapeDtypeStruct((n_q * HEADS * rows, n_kv * tokens), jnp.bfloat16),
            jax.ShapeDtypeStruct((n_q * rows, LANES), jnp.float32),
        ],
        in_specs=[VMEM_BLOCK] * (n_q + 2 * n_kv),
        out_specs=[VMEM_BLOCK] * 2,
        compiler_params=pltpu.CompilerParams(vmem_limit_bytes=24 << 20),
    )(*q_blocks, *k_blocks, *page_blocks)


def early_call(weights, v_blocks):
    return pl.pallas_call(
        early_kernel,
        out_shape=jax.ShapeDtypeStruct((weights.shape[0], 2 * LANES), jnp.float32),
        in_specs=[VMEM_BLOCK] * (1 + len(v_blocks)),
        out_specs=VMEM_BLOCK,
        compiler_params=pltpu.CompilerParams(vmem_limit_bytes=24 << 20),
    )(weights, *v_blocks)


def late_call(weights, tops, sums, v_block, n_q):
    rows = tops.shape[0] // n_q
    return pl.pallas_call(
        functools.partial(late_kernel, n_q),
        out_shape=[jax.ShapeDtypeStruct((rows, WIDTH + LANES), jnp.bfloat16)] * n_q,
        in_specs=[VMEM_BLOCK] * 4,
        out_specs=[VMEM_BLOCK] * n_q,
        compiler_params=pltpu.CompilerParams(vmem_limit_bytes=24 << 20),
    )(weights, tops, sums, v_block)


def stats_of(ref):
    stat = ref[:, WIDTH:].astype(jnp.float32)
    mass = pltpu.roll(stat, LANES - HEADS, 1) + pltpu.roll(stat, LANES - 2 * HEADS, 1)
    return stat, mass


def join_kernel(n, *refs):
    parts, sum_ref, stat_ref = refs[:n], refs[n], refs[n + 1]
    tops, masses = zip(*map(stats_of, parts))
    top = functools.reduce(jnp.maximum, tops)
    factors = [jnp.exp2((t - top) * EXP2_SCALE) for t in tops]
    stat_ref[:, :LANES] = top
    stat_ref[:, LANES:] = functools.reduce(
        jnp.add, [f * m for f, m in zip(factors, masses)]
    )
    for head in range(HEADS):
        at = slice(head * HEAD_DIM, (head + 1) * HEAD_DIM)
        sum_ref[:, at] = functools.reduce(
            jnp.add,
            [
                factor[:, head : head + 1] * ref[:, at].astype(jnp.float32)
                for factor, ref in zip(factors, parts)
            ],
        )


def merge_kernel(sum_ref, stat_ref, part_ref, out_ref):
    top, mass = stat_ref[:, :LANES], stat_ref[:, LANES:]
    part_top, part_mass = stats_of(part_ref)
    best = jnp.maximum(top, part_top)
    factor = jnp.exp2((top - best) * EXP2_SCALE)
    part_factor = jnp.exp2((part_top - best) * EXP2_SCALE)
    total = factor * mass + part_factor * part_mass
    share, part_share = factor / total, part_factor / total
    for head in range(HEADS):
        at = slice(head * HEAD_DIM, (head + 1) * HEAD_DIM)
        part = part_ref[:, at].astype(jnp.float32)
        value = share[:, head : head + 1] * sum_ref[:, at]
        value = value + part_share[:, head : head + 1] * part
        out_ref[:, at] = value.astype(jnp.bfloat16)


def join_call(parts):
    rows = parts[0].shape[0]
    return pl.pallas_call(
        functools.partial(join_kernel, len(parts)),
        out_shape=[
            jax.ShapeDtypeStruct((rows, WIDTH), jnp.float32),
            jax.ShapeDtypeStruct((rows, 2 * LANES), jnp.float32),
        ],
        in_specs=[VMEM_BLOCK] * len(parts),
        out_specs=[VMEM_BLOCK] * 2,
        compiler_params=pltpu.CompilerParams(vmem_limit_bytes=8 << 20),
    )(*parts)


def merge_call(sums, stats, part):
    return pl.pallas_call(
        merge_kernel,
        out_shape=jax.ShapeDtypeStruct(sums.shape, jnp.bfloat16),
        in_specs=[VMEM_BLOCK] * 3,
        out_specs=VMEM_BLOCK,
        compiler_params=pltpu.CompilerParams(vmem_limit_bytes=8 << 20),
    )(sums, stats, part)


def pooled(block, own):
    across = swapped(block, 2)
    beside = swapped(block, 1)
    return [own, beside, across, swapped(across, 1)]


def attend(queries, key_cache, value_cache, tile_page, row_last):
    groups = lax.axis_size("blk") // SHARE
    pages = tile_page.reshape(1, -1)
    own_q, own_k, own_v, own_page = stage_call(
        row_last, queries, key_cache, value_cache, pages
    )
    k_blocks = pooled(key_cache, own_k)
    v_blocks = pooled(value_cache, own_v)
    page_blocks = pooled(pages, own_page)
    q_blocks = [own_q] + [swapped(own_q, SHARE * d) for d in range(1, groups)]
    partials = []
    for start in range(0, groups, 4):
        some = q_blocks[start : start + 4]
        weights, tops = weights_call(some, k_blocks, page_blocks)
        sums = early_call(weights, v_blocks[:-1])
        partials += late_call(weights, tops, sums, v_blocks[-1], len(some))
    parts = [partials[0]] + [swapped(partials[d], SHARE * d) for d in range(1, groups)]
    sums, stats = join_call(parts[:2] + parts[3:])
    return merge_call(sums, stats, parts[2])


def solution(mesh):
    placed = (
        P(("parts", "blk"), None),
        P(("parts", "blk"), None),
        P(("parts", "blk"), None),
        P(("parts", "blk")),
        P(("parts", "blk")),
    )
    return jax.shard_map(
        attend, mesh=mesh, in_specs=placed, out_specs=P(("parts", "blk"), None), check_vma=False
    )
```
